256 devices in a mesh: img: 128 (over z, x, y), rep: 2 (over core).
Axes of the slice: x: 4, y: 4, z: 8, core: 2. Of those that a mesh axis runs over, the one named last changes fastest.
Arguments:
- panels: float32 [256, 512, 128], P('img', 'rep'), may hold values from -6 to 6
- blocks: bfloat16 [6144, 512, 512], P('img', None, 'rep'), may hold values from -0.25 to 0.25
- pairs: int32 [6144, 2], P('img'), may hold values from 0 to 255, as said below
- counts: int32 [128], P('img'), may hold values from 12 to 48, as said below
Outputs:
- basis: float32 [256, 512, 128], P('img', 'rep')
The draws below stay inside these ranges and needn't reach their ends.
Inputs may be any that keep to these rules, and one draw needn't show every extreme that they name: `pairs`: row d * 48 + s is slot s of index d of img: its first image is one of d * 2 to d * 2 + 1, its second image lies on one of the indices d + 1 to d + 8 modulo 128. At most 6 slots of one index name second images on one other index, and that many is reached. `counts`: some index of img has all 48 slots live.
All inputs are finite; a program needn't handle non-finite values.
Results may differ from the reference program's by a relative error of at most 0.0025.
The reference program's roundings to bfloat16 on the way (of `rounded` and `reverse`) count: a program that leaves them out, or rounds other values in their place, can miss the bound.
Values may be sent and summed in bfloat16 or wider, within the bound.
A program may use at most 128 MiB of HBM per device.

```python
import jax
import jax.numpy as jnp
from jax import lax

KEYPTS = 512
UNIV = 128
BAND = 8
IMG_DEV = 2
PAIR_DEV = 48
IMAGES = 256
PAIRS = 6144
N_IMG = 128


def draw_pairs(key, part):
    base = jax.random.fold_in(key, 17)
    order_key, first_key, second_key = jax.random.split(base, 3)
    orders = jax.vmap(lambda single: jax.random.permutation(single, BAND))(jax.random.split(order_key, N_IMG))
    slot_ids = jnp.arange(PAIR_DEV) % BAND
    device_ids = jnp.arange(N_IMG)[:, None]
    peers = (device_ids + 1 + orders[:, slot_ids]) % N_IMG
    first = device_ids * IMG_DEV + jax.random.randint(first_key, (N_IMG, PAIR_DEV), 0, IMG_DEV)
    second = peers * IMG_DEV + jax.random.randint(second_key, (N_IMG, PAIR_DEV), 0, IMG_DEV)
    return jnp.stack([first, second], axis=-1).reshape(N_IMG * PAIR_DEV, 2).astype(jnp.int32)


def draw_counts(key, part):
    base = jax.random.fold_in(key, 29)
    count_key, pick_key = jax.random.split(base, 2)
    drawn = jax.random.randint(count_key, (N_IMG,), PAIR_DEV // 4, PAIR_DEV + 1)
    chosen = jax.random.randint(pick_key, (), 0, N_IMG)
    drawn = jnp.where(jnp.arange(N_IMG) == chosen, PAIR_DEV, drawn)
    return drawn.astype(jnp.int32)


def levels(rng, dims, cuts, low, high):
    gain = 1.0
    for position, blocks in cuts:
        draws = jax.random.uniform(jax.random.fold_in(jax.random.fold_in(rng, 6), position), (blocks,), jnp.float32, low / len(cuts), high / len(cuts))
        gain = gain * jnp.repeat(jnp.exp(draws), dims[position] // blocks).reshape((-1,) + (1,) * (len(dims) - 1 - position))
    return gain


def gaussian(rng, extent, scale, limit, shards=(), kind=jnp.bfloat16):
    values = jax.random.normal(rng, extent, jnp.float32) * scale
    if len(shards) > 0:
        values = levels(rng, extent, shards, -0.22, 0.18) * values
    return jnp.clip(values, min=-limit, max=limit).astype(kind)


def setup_inputs(seed: int = 0) -> dict:
    keys = jax.random.split(jax.random.key(seed), 5)
    return {
        "panels": gaussian(keys[0], (IMAGES, KEYPTS, UNIV), 1.0, 6.0, ((0, 128), (1, 2)), jnp.float32),
        "blocks": gaussian(keys[1], (PAIRS, KEYPTS, KEYPTS), KEYPTS ** -0.5, 0.25, ((0, 128), (2, 2))),
        "pairs": draw_pairs(jax.random.fold_in(keys[4], 71), 0),
        "counts": draw_counts(jax.random.fold_in(keys[4], 71), 0),
    }


def reference(panels, blocks, pairs, counts):
    rounded = panels.astype(jnp.bfloat16)
    images_all = IMG_DEV * N_IMG
    slot_ids = jnp.arange(PAIR_DEV)

    def one_device(field, device):
        block_rows = lax.dynamic_slice_in_dim(blocks, device * PAIR_DEV, PAIR_DEV, 0).astype(jnp.float32)
        pair_rows = lax.dynamic_slice_in_dim(pairs, device * PAIR_DEV, PAIR_DEV, 0)
        alive_mask = (slot_ids < counts[device]).astype(jnp.float32)
        second_panels = rounded[pair_rows[:, 1]].astype(jnp.float32)
        first_panels = rounded[pair_rows[:, 0]].astype(jnp.float32)
        forward = jnp.einsum('skl,sln->skn', block_rows, second_panels)
        reverse = jnp.einsum('skl,skn->sln', block_rows, first_panels).astype(jnp.bfloat16)
        reverse = lax.optimization_barrier(reverse).astype(jnp.float32)
        field = field.at[pair_rows[:, 0]].add(forward * alive_mask[:, None, None])
        field = field.at[pair_rows[:, 1]].add(reverse * alive_mask[:, None, None])
        return (field, None)
    start_field = jnp.zeros((images_all, KEYPTS, UNIV), jnp.float32)
    field, _ = lax.scan(one_device, start_field, jnp.arange(N_IMG))
    field = panels + field
    gram_matrix = jnp.einsum('ikn,ikm->nm', field.astype(jnp.float32), field.astype(jnp.float32), precision=lax.Precision.HIGHEST, preferred_element_type=jnp.float32)
    gram_matrix = gram_matrix / (images_all * KEYPTS)
    factor = jnp.linalg.cholesky(gram_matrix)
    stacked = field.reshape(images_all * KEYPTS, UNIV)
    basis = lax.linalg.triangular_solve(factor, stacked, left_side=False, lower=True, transpose_a=True)
    return basis.reshape(images_all, KEYPTS, UNIV)
```

```python
import functools

import jax
import jax.numpy as jnp
from jax import lax
from jax.experimental import pallas as pl
from jax.experimental.pallas import tpu as pltpu
from jax.sharding import PartitionSpec as P

MESH = pl.DeviceIdType.MESH
BAND = 8
PLANE = 16
CHUNKS = 8
VMEM_LIMIT = 60 * 1024 * 1024


def remote(src, dst, send_sem, recv_sem, img, rep):
    return pltpu.make_async_remote_copy(
        src_ref=src,
        dst_ref=dst,
        send_sem=send_sem,
        recv_sem=recv_sem,
        device_id=(img, rep),
        device_id_type=MESH,
    )


def pair_tables(pairs, counts):
    slots = pairs.shape[0]
    capacity = slots // BAND
    devices = lax.axis_size("img")
    own = lax.axis_index("img")
    ids = jnp.arange(slots, dtype=jnp.int32)
    alive = ids < counts[0]
    first = pairs[:, 0] & 1
    second = pairs[:, 1] & 1
    offset = (pairs[:, 1] // 2 - own - 1) % devices
    same = (offset[:, None] == offset[None, :]) & (ids[None, :] < ids[:, None])
    rank = jnp.sum((same & alive[None, :]).astype(jnp.int32), axis=1)
    target = jnp.where(alive, offset * capacity + rank, slots)
    near_0 = jnp.where(second == 0, first, 2)
    near_1 = jnp.where(second == 1, first, 2)
    code = ids * 16 + near_0 * 4 + near_1
    hit = target[None, :] == ids[:, None]
    empty = 2 * 4 + 2
    placed = empty + jnp.sum(jnp.where(hit, code - empty, 0), axis=1)
    far = offset * 2 + second
    far_0 = jnp.where(alive & (first == 0), far, 2 * BAND)
    far_1 = jnp.where(alive & (first == 1), far, 2 * BAND)
    return jnp.stack([placed // 16, (placed // 4) % 4, placed % 4, far_0, far_1])


def field_kernel(
    table,
    panels,
    rounded,
    blocks_hbm,
    field,
    gram,
    blocks,
    far,
    near_other,
    near,
    turned,
    returned,
    part,
    part_other,
    load_sem,
    far_send,
    far_recv,
    near_send,
    near_recv,
    back_send,
    back_recv,
    part_send,
    part_recv,
):
    me = lax.axis_index("img")
    rep = lax.axis_index("rep")
    devices = lax.axis_size("img")
    slots, keypts, half = blocks.shape
    univ = panels.shape[2]
    capacity = slots // BAND
    step = slots // CHUNKS

    def load(chunk):
        rows = pl.ds(chunk * step, step)
        return pltpu.make_async_copy(blocks_hbm.at[rows], blocks.at[rows], load_sem.at[chunk])

    for chunk in range(CHUNKS):
        load(chunk).start()

    barrier = pltpu.get_barrier_semaphore()

    def greet(k, _):
        up = (me + k + 1) % devices
        down = (me + devices - k - 1) % devices
        pl.semaphore_signal(barrier, inc=1, device_id=(up, rep), device_id_type=MESH)
        pl.semaphore_signal(barrier, inc=1, device_id=(down, rep), device_id_type=MESH)
        return 0

    lax.fori_loop(0, BAND, greet, 0)
    pl.semaphore_signal(barrier, inc=1, device_id=(me, 1 - rep), device_id_type=MESH)
    pl.semaphore_wait(barrier, 2 * BAND + 1)

    near_copy = remote(rounded, near_other, near_send, near_recv, me, 1 - rep)
    near_copy.start()

    def far_copy(k):
        down = (me + devices - k - 1) % devices
        return remote(
            rounded, far.at[pl.ds(2 * k, 2)], far_send.at[k], far_recv.at[k], down, rep
        )

    def start_far(t, _):
        far_copy(BAND - 1 - t).start()
        return 0

    lax.fori_loop(0, BAND, start_far, 0)
    far[2 * BAND] = jnp.zeros((half, univ), far.dtype)
    near[2] = jnp.zeros((univ, keypts), near.dtype)
    here = pl.ds(pl.multiple_of(rep * half, half), half)
    there = pl.ds(pl.multiple_of((1 - rep) * half, half), half)
    for image in range(2):
        near[image, :, here] = panels[image].T.astype(near.dtype)
    near_copy.wait()
    for image in range(2):
        near[image, :, there] = near_other[image].astype(jnp.float32).T.astype(near.dtype)
    for chunk in range(CHUNKS):
        load(chunk).wait()

    def back_copy(k):
        up = (me + k + 1) % devices
        return remote(turned.at[k], returned.at[k], back_send.at[k], back_recv.at[k], up, rep)

    def reverse(t, _):
        k = BAND - 1 - t
        total = jnp.zeros((2 * univ, half), jnp.float32)
        for r in range(capacity):
            q = k * capacity + r
            block = blocks[table[0, q]]
            rows = jnp.concatenate([near[table[1, q]], near[table[2, q]]], axis=0)
            product = jnp.dot(rows, block, preferred_element_type=jnp.float32)
            total = total + product.astype(jnp.bfloat16).astype(jnp.float32)
        for image in range(2):
            own = total[image * univ : (image + 1) * univ]
            turned[k, image] = own.T.astype(turned.dtype)
        back_copy(k).start()
        return 0

    lax.fori_loop(0, BAND, reverse, 0)

    def wait_far(k, _):
        far_copy(k).wait_recv()
        return 0

    lax.fori_loop(0, BAND, wait_far, 0)

    group = 4

    def forward(rows, out):
        out[...] = jnp.zeros_like(out)

        def one(g, _):
            left = []
            right = []
            for r in range(group):
                s = g * group + r
                left.append(blocks[s, rows, :])
                right.append(jnp.concatenate([far[table[3, s]], far[table[4, s]]], axis=1))
            out[...] += jnp.dot(
                jnp.concatenate(left, axis=1),
                jnp.concatenate(right, axis=0),
                preferred_element_type=jnp.float32,
            )
            return 0

        lax.fori_loop(0, slots // group, one, 0)

    part_copy = remote(part.at[0], part_other, part_send, part_recv, me, 1 - rep)
    forward(there, part.at[0])
    part_copy.start()
    forward(here, part.at[1])
    part_copy.wait_recv()

    def wait_back(k, _):
        back_copy(k).wait_recv()
        return 0

    lax.fori_loop(0, BAND, wait_back, 0)

    total = jnp.zeros((univ, univ), jnp.float32)
    for image in range(2):
        columns = pl.ds(image * univ, univ)
        value = panels[image] + part[1, :, columns] + part_other[:, columns]
        for k in range(BAND):
            value = value + returned[k, image].astype(jnp.float32)
        field[image] = value
        total = total + lax.dot_general(
            value,
            value,
            (((0,), (0,)), ((), ())),
            precision=lax.Precision.HIGHEST,
            preferred_element_type=jnp.float32,
        )
    for r in range(gram.shape[0]):
        gram[r] = total[r * gram.shape[1] : (r + 1) * gram.shape[1]]


    def wait_sends(k, _):
        far_copy(k).wait_send()
        back_copy(k).wait_send()
        return 0

    lax.fori_loop(0, BAND, wait_sends, 0)
    part_copy.wait_send()


def field_and_gram(table, panels, rounded, blocks):
    slots, keypts, half = blocks.shape
    univ = panels.shape[2]
    pieces = 2 * PLANE
    dma = pltpu.SemaphoreType.DMA
    return pl.pallas_call(
        field_kernel,
        out_shape=(
            jax.ShapeDtypeStruct(panels.shape, jnp.float32),
            jax.ShapeDtypeStruct((pieces, univ // pieces, univ), jnp.float32),
        ),
        in_specs=[
            pl.BlockSpec(memory_space=pltpu.SMEM),
            pl.BlockSpec(memory_space=pltpu.VMEM),
            pl.BlockSpec(memory_space=pltpu.VMEM),
            pl.BlockSpec(memory_space=pl.ANY),
        ],
        out_specs=(
            pl.BlockSpec(memory_space=pltpu.VMEM),
            pl.BlockSpec(memory_space=pltpu.VMEM),
        ),
        scratch_shapes=[
            pltpu.VMEM((slots, keypts, half), jnp.bfloat16),
            pltpu.VMEM((2 * BAND + 1, half, univ), jnp.bfloat16),
            pltpu.VMEM((2, half, univ), jnp.bfloat16),
            pltpu.VMEM((3, univ, keypts), jnp.bfloat16),
            pltpu.VMEM((BAND, 2, half, univ), jnp.bfloat16),
            pltpu.VMEM((BAND, 2, half, univ), jnp.bfloat16),
            pltpu.VMEM((2, half, 2 * univ), jnp.float32),
            pltpu.VMEM((half, 2 * univ), jnp.float32),
            dma((CHUNKS,)),
            dma((BAND,)),
            dma((BAND,)),
            dma,
            dma,
            dma((BAND,)),
            dma((BAND,)),
            dma,
            dma,
        ],
        compiler_params=pltpu.CompilerParams(
            collective_id=0, has_side_effects=True, vmem_limit_bytes=VMEM_LIMIT
        ),
        name="field",
    )(table, panels, rounded, blocks)


def sum_kernel(gram, out, parts, plane_sums, pieces, s1, r1, s2, r2, s3, r3):
    me = lax.axis_index("img")
    rep = lax.axis_index("rep")
    devices = lax.axis_size("img")
    levels = devices // PLANE
    size = 2 * PLANE
    level = me // PLANE
    rank = (me % PLANE) * 2 + rep
    base = level * PLANE

    def in_plane(t):
        other = (rank + t) % size
        return other, base + other // 2, other % 2

    def over_levels(t):
        return ((level + t) % levels) * PLANE + me % PLANE

    barrier = pltpu.get_barrier_semaphore()

    def greet_plane(t, _):
        _, img, core = in_plane(t)
        pl.semaphore_signal(barrier, inc=1, device_id=(img, core), device_id_type=MESH)
        return 0

    def greet_level(t, _):
        pl.semaphore_signal(
            barrier, inc=1, device_id=(over_levels(t), rep), device_id_type=MESH
        )
        return 0

    lax.fori_loop(1, levels, greet_level, 0)
    lax.fori_loop(1, size, greet_plane, 0)
    pl.semaphore_wait(barrier, size - 1 + levels - 1)

    def scatter(t):
        other, img, core = in_plane(t)
        return remote(gram.at[other], parts.at[t - 1], s1.at[t - 1], r1.at[t - 1], img, core)

    def across(t):
        return remote(
            plane_sums.at[level],
            plane_sums.at[level],
            s2.at[t - 1],
            r2.at[t - 1],
            over_levels(t),
            rep,
        )

    def across_in(t):
        from_level = (level + levels - t) % levels
        return remote(
            plane_sums.at[from_level],
            plane_sums.at[from_level],
            s2.at[t - 1],
            r2.at[t - 1],
            over_levels(t),
            rep,
        )

    def gather(t):
        _, img, core = in_plane(t)
        return remote(pieces.at[rank], pieces.at[rank], s3.at[t - 1], r3.at[t - 1], img, core)

    def gather_in(t):
        from_rank = (rank + size - t) % size
        _, img, core = in_plane(t)
        return remote(
            pieces.at[from_rank], pieces.at[from_rank], s3.at[t - 1], r3.at[t - 1], img, core
        )

    def each(first, last, act):
        def body(t, _):
            act(t)
            return 0

        lax.fori_loop(first, last, body, 0)

    each(1, size, lambda t: scatter(t).start())
    each(1, size, lambda t: scatter(t).wait_recv())
    total = gram[rank]
    for t in range(size - 1):
        total = total + parts[t]
    plane_sums[level] = total
    each(1, levels, lambda t: across(t).start())
    each(1, levels, lambda t: across_in(t).wait_recv())
    total = plane_sums[0]
    for t in range(1, levels):
        total = total + plane_sums[t]
    pieces[rank] = total
    each(1, size, lambda t: gather(t).start())
    each(1, size, lambda t: gather_in(t).wait_recv())
    width = gram.shape[1]
    for r in range(size):
        out[r * width : (r + 1) * width] = pieces[r]
    each(1, size, lambda t: scatter(t).wait_send())
    each(1, levels, lambda t: across(t).wait_send())
    each(1, size, lambda t: gather(t).wait_send())


def summed_gram(gram):
    size, width, univ = gram.shape
    levels = lax.axis_size("img") // PLANE
    dma = pltpu.SemaphoreType.DMA
    return pl.pallas_call(
        sum_kernel,
        out_shape=jax.ShapeDtypeStruct((size * width, univ), jnp.float32),
        in_specs=[pl.BlockSpec(memory_space=pltpu.VMEM)],
        out_specs=pl.BlockSpec(memory_space=pltpu.VMEM),
        scratch_shapes=[
            pltpu.VMEM((size - 1, width, univ), jnp.float32),
            pltpu.VMEM((levels, width, univ), jnp.float32),
            pltpu.VMEM((size, width, univ), jnp.float32),
            dma((size - 1,)),
            dma((size - 1,)),
            dma((levels - 1,)),
            dma((levels - 1,)),
            dma((size - 1,)),
            dma((size - 1,)),
        ],
        compiler_params=pltpu.CompilerParams(collective_id=1, has_side_effects=True),
        name="sum_gram",
    )(gram)


def basis_kernel(scale, gram, field, basis):
    univ = gram.shape[0]
    left = gram[...] * scale
    rows = lax.broadcasted_iota(jnp.int32, (univ, univ), 0)
    columns = lax.broadcasted_iota(jnp.int32, (univ, univ), 1)
    unit = (rows == columns).astype(jnp.float32)
    right = unit
    diagonal = jnp.zeros((univ, univ), jnp.float32)
    for j in range(univ):
        top = (j // 8) * 8
        low = left[top:]
        low_right = right[top:]
        row = low[j - top : j - top + 1]
        row_right = low_right[j - top : j - top + 1]
        pivot = row[:, j : j + 1]
        inverse = 1.0 / pivot
        below = rows[top:] > j
        factor = jnp.where(below, low[:, j : j + 1] * inverse, 0.0)
        diagonal = jnp.where(rows == j, lax.rsqrt(pivot), diagonal)
        low = low - factor * row
        low_right = low_right - factor * row_right
        left = jnp.concatenate([left[:top], low], axis=0) if top else low
        right = jnp.concatenate([right[:top], low_right], axis=0) if top else low_right
    inverse_factor = right * diagonal
    for image in range(field.shape[0]):
        basis[image] = lax.dot_general(
            field[image],
            inverse_factor,
            (((1,), (1,)), ((), ())),
            precision=lax.Precision.HIGHEST,
            preferred_element_type=jnp.float32,
        )


def shards(panels, blocks, pairs, counts):
    table = pair_tables(pairs, counts)
    rounded = panels.astype(jnp.bfloat16)
    field, gram = field_and_gram(table, panels, rounded, blocks)
    gram = summed_gram(gram)
    rows = lax.axis_size("img") * panels.shape[0] * lax.axis_size("rep") * panels.shape[1]
    return pl.pallas_call(
        functools.partial(basis_kernel, 1.0 / rows),
        out_shape=jax.ShapeDtypeStruct(panels.shape, jnp.float32),
        in_specs=[pl.BlockSpec(memory_space=pltpu.VMEM)] * 2,
        out_specs=pl.BlockSpec(memory_space=pltpu.VMEM),
        name="basis",
    )(gram, field)


def solution(mesh):
    in_specs = (P("img", "rep", None), P("img", None, "rep"), P("img", None), P("img"))
    out_specs = P("img", "rep", None)
    return jax.shard_map(shards, mesh=mesh, in_specs=in_specs, out_specs=out_specs, check_vma=False)
```

```python
import functools

import jax
import jax.numpy as jnp
from jax import lax
from jax.experimental import pallas as pl
from jax.experimental.pallas import tpu as pltpu
from jax.sharding import PartitionSpec as P

MESH = pl.DeviceIdType.MESH
BAND = 8
SIDE = 4
PLANE = SIDE * SIDE
PIVOTS = 4
RELAY_MIDDLE = 1
RELAY_LAST = 5
CHUNKS = 8
VMEM_LIMIT = 60 * 1024 * 1024


def remote(src, dst, send_sem, recv_sem, img, rep):
    return pltpu.make_async_remote_copy(
        src_ref=src,
        dst_ref=dst,
        send_sem=send_sem,
        recv_sem=recv_sem,
        device_id=(img, rep),
        device_id_type=MESH,
    )


def pair_tables(pairs, counts):
    slots = pairs.shape[0]
    capacity = slots // BAND
    devices = lax.axis_size("img")
    own = lax.axis_index("img")
    ids = jnp.arange(slots, dtype=jnp.int32)
    alive = ids < counts[0]
    first = pairs[:, 0] & 1
    second = pairs[:, 1] & 1
    offset = (pairs[:, 1] // 2 - own - 1) % devices
    same = (offset[:, None] == offset[None, :]) & (ids[None, :] < ids[:, None])
    rank = jnp.sum((same & alive[None, :]).astype(jnp.int32), axis=1)
    target = jnp.where(alive, offset * capacity + rank, slots)
    code = ids * 8 + first * 2 + second
    hit = target[None, :] == ids[:, None]
    empty = 2 * 2
    placed = empty + jnp.sum(jnp.where(hit, code - empty, 0), axis=1)
    far = offset * 2 + second
    far_0 = jnp.where(alive & (first == 0), far, 2 * BAND + 2)
    far_1 = jnp.where(alive & (first == 1), far, 2 * BAND + 2)
    return jnp.stack([placed // 8, (placed // 2) % 4, placed % 2, far_0, far_1])


def each(first, last, act):
    def body(t, _):
        act(t)
        return 0

    lax.fori_loop(first, last, body, 0)


def field_kernel(
    table,
    panels,
    blocks_hbm,
    field,
    gram,
    blocks,
    far,
    near_other,
    near,
    turned,
    returned,
    sums,
    raised,
    lifted,
    part,
    part_other,
    local,
    corner_parts,
    column,
    levels,
    pieces,
    load_sem,
    far_send,
    far_recv,
    near_send,
    near_recv,
    back_send,
    back_recv,
    up_send,
    up_recv,
    part_send,
    part_recv,
    s1,
    r1,
    s2,
    r2,
    s3,
    r3,
    s4,
    r4,
):
    me = lax.axis_index("img")
    rep = lax.axis_index("rep")
    devices = lax.axis_size("img")
    slots, keypts, half = blocks.shape
    univ = panels.shape[2]
    capacity = slots // BAND
    step = slots // CHUNKS
    height = devices // PLANE
    z = me // PLANE
    x = (me // SIDE) % SIDE
    y = me % SIDE
    above = (me + SIDE) % devices
    below = (me + devices - SIDE) % devices
    own_row = 2 * BAND
    zero_row = 2 * BAND + 2

    def load(chunk):
        rows = pl.ds(chunk * step, step)
        return pltpu.make_async_copy(blocks_hbm.at[rows], blocks.at[rows], load_sem.at[chunk])

    for chunk in range(CHUNKS):
        load(chunk).start()

    rank = y * 2 + rep

    def in_corner(t):
        other = (rank + t) % (2 * SIDE)
        return other, me - y + other // 2, other % 2

    def in_column(t):
        other = (x + t) % SIDE
        return other, z * PLANE + other * SIDE + y

    def in_levels(t):
        return ((z + t) % height) * PLANE + me % PLANE

    barrier = pltpu.get_barrier_semaphore()

    def greet(img, core):
        pl.semaphore_signal(barrier, inc=1, device_id=(img, core), device_id_type=MESH)

    def greet_corner(t):
        _, img, core = in_corner(t)
        greet(img, core)

    each(1, height, lambda t: greet(in_levels(t), rep))
    each(1, 2 * SIDE, greet_corner)
    each(1, SIDE, lambda t: greet(in_column(t)[1], rep))
    greet(above, rep)
    greet(below, rep)

    here = pl.ds(pl.multiple_of(rep * half, half), half)
    there = pl.ds(pl.multiple_of((1 - rep) * half, half), half)
    for image in range(2):
        far[own_row + image] = panels[image].astype(far.dtype)
        near[image, :, here] = panels[image].T.astype(near.dtype)
    far[zero_row] = jnp.zeros((half, univ), far.dtype)
    near[2] = jnp.zeros((univ, keypts), near.dtype)

    pl.semaphore_wait(barrier, height - 1 + 2 * SIDE - 1 + SIDE - 1 + 2)

    def far_rows(slot):
        return far.at[pl.ds(2 * slot, 2)]

    def mate(dy):
        return me - y + (y + dy) % SIDE

    def down(source, slot, sem):
        return remote(far_rows(source), far_rows(slot), far_send.at[sem], far_recv.at[slot], below, rep)

    def side(source, slot, sem, dy):
        return remote(
            far_rows(source), far_rows(slot), far_send.at[sem], far_recv.at[slot], mate(dy), rep
        )

    def own_side(dy):
        return side(BAND, 3 - dy, 1 + dy, dy)

    def middle_side(dy):
        return side(3, jnp.where(y + dy < SIDE, 3 - dy, 7 - dy), 4 + dy, dy)

    def last_side(dy):
        return side(7, 7 - dy, 7 + dy, dy)

    near_copy = remote(
        far_rows(BAND), near_other, near_send, near_recv, me, 1 - rep
    )
    near_copy.start()
    first_down = down(BAND, 3, 0)
    second_down = down(3, 7, 1)
    first_down.start()
    for dy in range(1, SIDE):

        @pl.when(y + dy >= SIDE)
        def _():
            own_side(dy).start()

    near_copy.wait()
    for image in range(2):
        near[image, :, there] = near_other[image].astype(jnp.float32).T.astype(near.dtype)
    for chunk in range(CHUNKS):
        load(chunk).wait()

    def back_copy(k):
        return remote(
            turned.at[k - 1],
            returned.at[k - 1],
            back_send.at[k - 1],
            back_recv.at[k - 1],
            mate(k % SIDE),
            rep,
        )

    def reverse(t):
        k = BAND - t
        totals = [jnp.zeros((univ, half), jnp.float32) for _ in range(2)]
        for r in range(capacity):
            q = (k - 1) * capacity + r
            product = jnp.dot(
                near[table[1, q]], blocks[table[0, q]], preferred_element_type=jnp.float32
            )
            product = product.astype(jnp.bfloat16).astype(jnp.float32)
            share = table[2, q].astype(jnp.float32)
            totals[0] = totals[0] + product * (1.0 - share)
            totals[1] = totals[1] + product * share
        for image in range(2):
            turned[k - 1, image] = totals[image].T.astype(turned.dtype)

        @pl.when(k % SIDE != 0)
        def _():
            back_copy(k).start()

    def relay_middle():
        far_wait(3)
        second_down.start()
        for dy in range(1, SIDE):
            middle_side(dy).start()

    def relay_last():
        far_wait(7)
        for dy in range(1, SIDE):

            @pl.when(y + dy < SIDE)
            def _():
                last_side(dy).start()

    def far_wait(slot):
        remote(
            far_rows(slot), far_rows(slot), far_send.at[0], far_recv.at[slot], below, rep
        ).wait_recv()

    def reverse_and_relay(t):
        reverse(t)

        @pl.when(t == RELAY_MIDDLE)
        def _():
            relay_middle()

        @pl.when(t == RELAY_LAST)
        def _():
            relay_last()

    each(0, BAND, reverse_and_relay)

    def add(slot, source, k):
        for image in range(2):
            sums[slot, image] += source[k, image].astype(jnp.float32)

    def lift(slot, which):
        for image in range(2):
            raised[which, image] = sums[slot, image].astype(raised.dtype)
        return up(which)

    def up(which):
        return remote(
            raised.at[which], lifted.at[which], up_send.at[which], up_recv.at[which], above, rep
        )

    def back_wait(k):
        back_copy(k).wait_recv()

    for image in range(2):
        sums[0, image] = jnp.zeros((half, univ), jnp.float32)
        sums[1, image] = turned[3, image].astype(jnp.float32)
        sums[2, image] = turned[7, image].astype(jnp.float32)

    for dy in range(1, SIDE):
        back_wait(4 + dy)
        add(jnp.where(y >= dy, 1, 2), returned, 3 + dy)
    lift(2, 0).start()

    for slot in (0, 1, 2, 4, 5, 6):
        far_wait(slot)

    group = 8

    def forward(rows, out):
        out[...] = jnp.zeros_like(out)

        def one(g):
            left = []
            right = []
            for r in range(group):
                s = g * group + r
                left.append(blocks[s, rows, :])
                right.append(jnp.concatenate([far[table[3, s]], far[table[4, s]]], axis=1))
            out[...] += jnp.dot(
                jnp.concatenate(left, axis=1),
                jnp.concatenate(right, axis=0),
                preferred_element_type=jnp.float32,
            )

        each(0, slots // group, one)

    part_copy = remote(part.at[0], part_other, part_send, part_recv, me, 1 - rep)
    forward(there, part.at[0])
    part_copy.start()

    for dy in range(1, SIDE):
        back_wait(dy)
        add(jnp.where(y >= dy, 0, 1), returned, dy - 1)
    up(0).wait_recv()
    add(1, lifted, 0)
    lift(1, 1).start()

    forward(here, part.at[1])
    part_copy.wait_recv()
    up(1).wait_recv()

    total = jnp.zeros((univ, univ), jnp.float32)
    for image in range(2):
        columns = pl.ds(image * univ, univ)
        value = panels[image] + part[1, :, columns] + part_other[:, columns]
        value = value + sums[0, image] + lifted[1, image].astype(jnp.float32)
        field[image] = value
        total = total + lax.dot_general(
            value,
            value,
            (((0,), (0,)), ((), ())),
            precision=lax.Precision.HIGHEST,
            preferred_element_type=jnp.float32,
        )

    width = local.shape[1]
    for r in range(2 * SIDE):
        local[r] = total[r * width : (r + 1) * width]

    def scatter_corner(t):
        other, img, core = in_corner(t)
        return remote(local.at[other], corner_parts.at[t - 1], s1.at[t - 1], r1.at[t - 1], img, core)

    def along_column(t, source):
        _, img = in_column(t)
        return remote(column.at[source], column.at[source], s2.at[t - 1], r2.at[t - 1], img, rep)

    def across(t, source):
        return remote(
            levels.at[source], levels.at[source], s3.at[t - 1], r3.at[t - 1], in_levels(t), rep
        )

    def gather_corner(t, source):
        _, img, core = in_corner(t)
        return remote(
            pieces.at[source], pieces.at[source], s4.at[t - 1], r4.at[t - 1], img, core
        )

    each(1, 2 * SIDE, lambda t: scatter_corner(t).start())
    each(1, 2 * SIDE, lambda t: scatter_corner(t).wait_recv())
    line = local[rank]
    for t in range(2 * SIDE - 1):
        line = line + corner_parts[t]
    column[x] = line
    each(1, SIDE, lambda t: along_column(t, x).start())
    each(1, SIDE, lambda t: along_column(t, (x + SIDE - t) % SIDE).wait_recv())
    line = column[0]
    for t in range(1, SIDE):
        line = line + column[t]
    levels[z] = line
    each(1, height, lambda t: across(t, z).start())
    each(1, height, lambda t: across(t, (z + height - t) % height).wait_recv())
    line = levels[0]
    for t in range(1, height):
        line = line + levels[t]
    pieces[rank] = line
    each(1, 2 * SIDE, lambda t: gather_corner(t, rank).start())
    each(1, 2 * SIDE, lambda t: gather_corner(t, (rank + 2 * SIDE - t) % (2 * SIDE)).wait_recv())
    for r in range(2 * SIDE):
        gram[r * width : (r + 1) * width] = pieces[r]

    first_down.wait_send()
    second_down.wait_send()
    for dy in range(1, SIDE):
        middle_side(dy).wait_send()

        @pl.when(y + dy >= SIDE)
        def _():
            own_side(dy).wait_send()

        @pl.when(y + dy < SIDE)
        def _():
            last_side(dy).wait_send()

        back_copy(dy).wait_send()
        back_copy(4 + dy).wait_send()
    up(0).wait_send()
    up(1).wait_send()
    part_copy.wait_send()
    each(1, 2 * SIDE, lambda t: scatter_corner(t).wait_send())
    each(1, SIDE, lambda t: along_column(t, x).wait_send())
    each(1, height, lambda t: across(t, z).wait_send())
    each(1, 2 * SIDE, lambda t: gather_corner(t, rank).wait_send())


def field_and_gram(table, panels, blocks):
    slots, keypts, half = blocks.shape
    univ = panels.shape[2]
    height = lax.axis_size("img") // PLANE
    line = 2 * SIDE
    width = univ // line
    dma = pltpu.SemaphoreType.DMA
    return pl.pallas_call(
        field_kernel,
        out_shape=(
            jax.ShapeDtypeStruct(panels.shape, jnp.float32),
            jax.ShapeDtypeStruct((univ, univ), jnp.float32),
        ),
        in_specs=[
            pl.BlockSpec(memory_space=pltpu.SMEM),
            pl.BlockSpec(memory_space=pltpu.VMEM),
            pl.BlockSpec(memory_space=pl.ANY),
        ],
        out_specs=(
            pl.BlockSpec(memory_space=pltpu.VMEM),
            pl.BlockSpec(memory_space=pltpu.VMEM),
        ),
        scratch_shapes=[
            pltpu.VMEM((slots, keypts, half), jnp.bfloat16),
            pltpu.VMEM((2 * BAND + 3, half, univ), jnp.bfloat16),
            pltpu.VMEM((2, half, univ), jnp.bfloat16),
            pltpu.VMEM((3, univ, keypts), jnp.bfloat16),
            pltpu.VMEM((BAND, 2, half, univ), jnp.bfloat16),
            pltpu.VMEM((BAND - 1, 2, half, univ), jnp.bfloat16),
            pltpu.VMEM((3, 2, half, univ), jnp.float32),
            pltpu.VMEM((2, 2, half, univ), jnp.bfloat16),
            pltpu.VMEM((2, 2, half, univ), jnp.bfloat16),
            pltpu.VMEM((2, half, 2 * univ), jnp.float32),
            pltpu.VMEM((half, 2 * univ), jnp.float32),
            pltpu.VMEM((line, width, univ), jnp.float32),
            pltpu.VMEM((line - 1, width, univ), jnp.float32),
            pltpu.VMEM((SIDE, width, univ), jnp.float32),
            pltpu.VMEM((height, width, univ), jnp.float32),
            pltpu.VMEM((line, width, univ), jnp.float32),
            dma((CHUNKS,)),
            dma((11,)),
            dma((BAND,)),
            dma,
            dma,
            dma((BAND - 1,)),
            dma((BAND - 1,)),
            dma((2,)),
            dma((2,)),
            dma,
            dma,
        ]
        + [dma((n - 1,)) for n in (line, SIDE, height, line) for _ in range(2)],
        compiler_params=pltpu.CompilerParams(
            collective_id=0, has_side_effects=True, vmem_limit_bytes=VMEM_LIMIT
        ),
        name="field",
    )(table, panels, blocks)


def basis_kernel(scale, gram, field, basis):
    univ = gram.shape[0]
    left = gram[...] * scale
    rows = lax.broadcasted_iota(jnp.int32, (univ, univ), 0)
    columns = lax.broadcasted_iota(jnp.int32, (univ, univ), 1)
    right = (rows == columns).astype(jnp.float32)
    scales = jnp.zeros((univ, univ), jnp.float32)
    for j in range(0, univ, PIVOTS):
        top = (j // 8) * 8
        at = j - top
        low = left[top:]
        low_right = right[top:]
        low_rows = rows[top:]
        unit = [[None] * PIVOTS for _ in range(PIVOTS)]
        pivots = []
        inverses = []
        for t in range(PIVOTS):
            entry = [
                jnp.broadcast_to(low[at + a : at + a + 1, j + t : j + t + 1], (1, univ))
                for a in range(t, PIVOTS)
            ]
            for u in range(t):
                for a in range(t, PIVOTS):
                    entry[a - t] = entry[a - t] - unit[a][u] * (unit[t][u] * pivots[u])
            pivots.append(entry[0])
            inverses.append(1.0 / entry[0])
            for a in range(t + 1, PIVOTS):
                unit[a][t] = entry[a - t] * inverses[t]
        row = []
        row_right = []
        factor = []
        for t in range(PIVOTS):
            one = low[at + t : at + t + 1]
            one_right = low_right[at + t : at + t + 1]
            column = jnp.broadcast_to(low[:, j + t : j + t + 1], low.shape)
            for u in range(t):
                one = one - unit[t][u] * row[u]
                one_right = one_right - unit[t][u] * row_right[u]
                column = column - factor[u] * (unit[t][u] * pivots[u])
            row.append(one)
            row_right.append(one_right)
            factor.append(column * inverses[t])
        below = low_rows >= j + PIVOTS
        for t in range(PIVOTS):
            share = jnp.where(below, factor[t], 0.0)
            low = low - share * row[t]
            low_right = low_right - share * row_right[t]
            scales = jnp.where(rows == j + t, lax.rsqrt(pivots[t]), scales)
        for t in range(1, PIVOTS):
            low_right = jnp.where(low_rows == j + t, row_right[t], low_right)
        left = jnp.concatenate([left[:top], low], axis=0) if top else low
        right = jnp.concatenate([right[:top], low_right], axis=0) if top else low_right
    inverse_factor = right * scales
    for image in range(field.shape[0]):
        basis[image] = lax.dot_general(
            field[image],
            inverse_factor,
            (((1,), (1,)), ((), ())),
            precision=lax.Precision.HIGHEST,
            preferred_element_type=jnp.float32,
        )


def shards(panels, blocks, pairs, counts):
    table = pair_tables(pairs, counts)
    field, gram = field_and_gram(table, panels, blocks)
    rows = lax.axis_size("img") * panels.shape[0] * lax.axis_size("rep") * panels.shape[1]
    return pl.pallas_call(
        functools.partial(basis_kernel, 1.0 / rows),
        out_shape=jax.ShapeDtypeStruct(panels.shape, jnp.float32),
        in_specs=[pl.BlockSpec(memory_space=pltpu.VMEM)] * 2,
        out_specs=pl.BlockSpec(memory_space=pltpu.VMEM),
        name="basis",
    )(gram, field)


def solution(mesh):
    in_specs = (P("img", "rep", None), P("img", None, "rep"), P("img", None), P("img"))
    out_specs = P("img", "rep", None)
    return jax.shard_map(shards, mesh=mesh, in_specs=in_specs, out_specs=out_specs, check_vma=False)
```

```python
import functools

import jax
import jax.numpy as jnp
from jax import lax
from jax.experimental import pallas as pl
from jax.experimental.pallas import tpu as pltpu
from jax.sharding import PartitionSpec as P

MESH = pl.DeviceIdType.MESH
BAND = 8
SIDE = 4
PLANE = SIDE * SIDE
PIVOTS = 4
EMPTY = 4
ORDER = (6, 7, 5, 3, 1, 8, 2, 4)
CHUNKS = 8
VMEM_LIMIT = 60 * 1024 * 1024


def remote(src, dst, send_sem, recv_sem, img, rep):
    return pltpu.make_async_remote_copy(
        src_ref=src,
        dst_ref=dst,
        send_sem=send_sem,
        recv_sem=recv_sem,
        device_id=(img, rep),
        device_id_type=MESH,
    )


def pair_codes(pairs, counts):
    slots = pairs.shape[0]
    capacity = slots // BAND
    devices = lax.axis_size("img")
    own = lax.axis_index("img")
    ids = jnp.arange(slots, dtype=jnp.int32)
    alive = ids < counts[0]
    offset = (pairs[:, 1] // 2 - own - 1) % devices
    same = (offset[:, None] == offset[None, :]) & (ids[None, :] < ids[:, None])
    rank = jnp.sum((same & alive[None, :]).astype(jnp.int32), axis=1)
    target = jnp.where(alive, offset * capacity + rank, slots)
    code = ids * 8 + (pairs[:, 0] & 1) * 2 + (pairs[:, 1] & 1)
    hit = target[None, :] == ids[:, None]
    return EMPTY + jnp.sum(jnp.where(hit, code[None, :] - EMPTY, 0), axis=1)


def each(first, last, act):
    def body(t, _):
        act(t)
        return 0

    lax.fori_loop(first, last, body, 0)


def field_kernel(
    codes,
    panels,
    blocks_hbm,
    field,
    gram,
    blocks,
    far,
    beyond,
    near_other,
    near,
    turned,
    returned,
    sums,
    raised,
    lifted,
    part,
    part_other,
    local,
    corner_parts,
    column,
    levels,
    pieces,
    load_sem,
    far_send,
    far_recv,
    near_send,
    near_recv,
    back_send,
    back_recv,
    up_send,
    up_recv,
    part_send,
    part_recv,
    s1,
    r1,
    s2,
    r2,
    s3,
    r3,
    s4,
    r4,
):
    me = lax.axis_index("img")
    rep = lax.axis_index("rep")
    devices = lax.axis_size("img")
    slots, keypts, half = blocks.shape
    univ = panels.shape[2]
    capacity = slots // BAND
    step = slots // CHUNKS
    height = devices // PLANE
    z = me // PLANE
    x = (me // SIDE) % SIDE
    y = me % SIDE
    above = (me + SIDE) % devices
    below = (me + devices - SIDE) % devices
    own_row = 2 * SIDE
    zero_row = 2 * SIDE + 2

    def read(q):
        code = codes[q]
        return code // 8, (code // 2) % 4, code % 2

    def load(chunk):
        rows = pl.ds(chunk * step, step)
        return pltpu.make_async_copy(blocks_hbm.at[rows], blocks.at[rows], load_sem.at[chunk])

    for chunk in range(CHUNKS):
        load(chunk).start()

    rank = y * 2 + rep

    def in_corner(t):
        other = (rank + t) % (2 * SIDE)
        return other, me - y + other // 2, other % 2

    def in_column(t):
        other = (x + t) % SIDE
        return other, z * PLANE + other * SIDE + y

    def in_levels(t):
        return ((z + t) % height) * PLANE + me % PLANE

    barrier = pltpu.get_barrier_semaphore()

    def greet(img, core):
        pl.semaphore_signal(barrier, inc=1, device_id=(img, core), device_id_type=MESH)

    def greet_corner(t):
        _, img, core = in_corner(t)
        greet(img, core)

    each(1, height, lambda t: greet(in_levels(t), rep))
    each(1, 2 * SIDE, greet_corner)
    each(1, SIDE, lambda t: greet(in_column(t)[1], rep))
    greet(above, rep)
    greet(below, rep)

    here = pl.ds(pl.multiple_of(rep * half, half), half)
    there = pl.ds(pl.multiple_of((1 - rep) * half, half), half)
    for image in range(2):
        far[own_row + image] = panels[image].astype(far.dtype)
        near[image, :, here] = panels[image].T.astype(near.dtype)
    far[zero_row] = jnp.zeros((half, univ), far.dtype)
    beyond[zero_row] = jnp.zeros((half, univ), far.dtype)
    near[2] = jnp.zeros((univ, keypts), near.dtype)

    pl.semaphore_wait(barrier, height - 1 + 2 * SIDE - 1 + SIDE - 1 + 2)

    def rows_of(buffer, slot):
        return buffer.at[pl.ds(2 * slot, 2)]

    def mate(dy):
        return me - y + (y + dy) % SIDE

    first_down = remote(
        rows_of(far, SIDE), rows_of(far, SIDE - 1), far_send.at[0], far_recv.at[SIDE - 1], below, rep
    )

    def next_down(slot):
        return remote(
            rows_of(far, slot),
            rows_of(beyond, slot),
            far_send.at[1 + slot],
            far_recv.at[SIDE + slot],
            below,
            rep,
        )

    def side(source, dy):
        slot = SIDE - 1 - dy
        return remote(
            rows_of(far, source),
            rows_of(far, slot),
            far_send.at[SIDE + dy],
            far_recv.at[slot],
            mate(dy),
            rep,
        )

    near_copy = remote(rows_of(far, SIDE), near_other, near_send, near_recv, me, 1 - rep)
    near_copy.start()
    first_down.start()
    for dy in range(1, SIDE):

        @pl.when(y + dy >= SIDE)
        def _():
            side(SIDE, dy).start()

    near_copy.wait()
    for image in range(2):
        near[image, :, there] = near_other[image].astype(jnp.float32).T.astype(near.dtype)
    for chunk in range(CHUNKS):
        load(chunk).wait()

    def back_copy(k, source):
        return remote(
            source,
            returned.at[k - 1],
            back_send.at[k - 1],
            back_recv.at[k - 1],
            mate(k % SIDE),
            rep,
        )

    def up(which, source):
        return remote(source, lifted.at[which], up_send.at[which], up_recv.at[which], above, rep)

    def reverse(t):
        k = ORDER[-1]
        for at in range(BAND - 1):
            k = jnp.where(t == at, ORDER[at], k)
        totals = [jnp.zeros((univ, half), jnp.float32) for _ in range(2)]
        for r in range(capacity):
            slot, first, second = read((k - 1) * capacity + r)
            product = jnp.dot(near[first], blocks[slot], preferred_element_type=jnp.float32)
            product = product.astype(jnp.bfloat16).astype(jnp.float32)
            share = second.astype(jnp.float32)
            totals[0] = totals[0] + product * (1.0 - share)
            totals[1] = totals[1] + product * share
        for image in range(2):
            turned[k - 1, image] = totals[image].T.astype(turned.dtype)

        @pl.when(k % 2 == 1)
        def _():
            back_copy(k, turned.at[k - 1]).start()

        @pl.when(k == 6)
        def _():
            up(2, turned.at[k - 1]).start()

    each(0, BAND, reverse)

    def far_wait(slot):
        remote(
            rows_of(far, SIDE - 1),
            rows_of(far, SIDE - 1),
            far_send.at[0],
            far_recv.at[slot],
            below,
            rep,
        ).wait_recv()

    far_wait(SIDE - 1)
    next_down(SIDE - 1).start()
    for dy in range(1, SIDE):

        @pl.when(y + dy < SIDE)
        def _():
            side(SIDE - 1, dy).start()

    up(2, raised.at[2]).wait_recv()
    for image in range(2):
        value = turned[1, image].astype(jnp.float32) + lifted[2, image].astype(jnp.float32)
        raised[2, image] = value.astype(raised.dtype)
    back_copy(2, raised.at[2]).start()
    for slot in range(SIDE - 2, -1, -1):
        far_wait(slot)
        next_down(slot).start()

    def add(slot, source, k):
        for image in range(2):
            sums[slot, image] += source[k, image].astype(jnp.float32)

    def lift(slot, which):
        for image in range(2):
            raised[which, image] = sums[slot, image].astype(raised.dtype)
        up(which, raised.at[which]).start()

    def back_wait(k):
        back_copy(k, raised.at[2]).wait_recv()

    for image in range(2):
        sums[0, image] = jnp.zeros((half, univ), jnp.float32)
        sums[1, image] = turned[3, image].astype(jnp.float32)
        sums[2, image] = turned[7, image].astype(jnp.float32)

    for dy in (1, 3):
        back_wait(4 + dy)
        add(jnp.where(y >= dy, 1, 2), returned, 3 + dy)
    lift(2, 0)

    group = 8

    def forward(rows, out, panel_buffer, offset, first_group):
        def one(g):
            left = []
            right = []
            for r in range(group):
                place = g * group + r
                slot, first, second = read(offset * capacity + place)
                row = (place // capacity) * 2 + second
                left.append(blocks[slot, rows, :])
                right.append(
                    jnp.concatenate(
                        [
                            panel_buffer[jnp.where(first == image, row, zero_row)]
                            for image in range(2)
                        ],
                        axis=1,
                    )
                )
            out[...] += jnp.dot(
                jnp.concatenate(left, axis=1),
                jnp.concatenate(right, axis=0),
                preferred_element_type=jnp.float32,
            )

        if first_group:
            out[...] = jnp.zeros_like(out)
        each(0, SIDE * capacity // group, one)

    part_copy = remote(part.at[0], part_other, part_send, part_recv, me, 1 - rep)
    forward(there, part.at[0], far, 0, True)
    forward(here, part.at[1], far, 0, True)

    for dy in range(1, SIDE):
        back_wait(dy)
        add(jnp.where(y >= dy, 0, 1), returned, dy - 1)
    up(0, raised.at[0]).wait_recv()
    add(1, lifted, 0)
    lift(1, 1)

    for slot in range(SIDE, BAND):
        far_wait(slot)
    forward(there, part.at[0], beyond, SIDE, False)
    part_copy.start()
    forward(here, part.at[1], beyond, SIDE, False)
    part_copy.wait_recv()
    up(1, raised.at[1]).wait_recv()

    total = jnp.zeros((univ, univ), jnp.float32)
    for image in range(2):
        columns = pl.ds(image * univ, univ)
        value = panels[image] + part[1, :, columns] + part_other[:, columns]
        value = value + sums[0, image] + lifted[1, image].astype(jnp.float32)
        field[image] = value
        total = total + lax.dot_general(
            value,
            value,
            (((0,), (0,)), ((), ())),
            precision=lax.Precision.HIGHEST,
            preferred_element_type=jnp.float32,
        )

    width = local.shape[1]
    for r in range(2 * SIDE):
        local[r] = total[r * width : (r + 1) * width]

    def scatter_corner(t):
        other, img, core = in_corner(t)
        return remote(local.at[other], corner_parts.at[t - 1], s1.at[t - 1], r1.at[t - 1], img, core)

    def along_column(t, source):
        _, img = in_column(t)
        return remote(column.at[source], column.at[source], s2.at[t - 1], r2.at[t - 1], img, rep)

    def across(t, source):
        return remote(
            levels.at[source], levels.at[source], s3.at[t - 1], r3.at[t - 1], in_levels(t), rep
        )

    def gather_corner(t, source):
        _, img, core = in_corner(t)
        return remote(
            pieces.at[source], pieces.at[source], s4.at[t - 1], r4.at[t - 1], img, core
        )

    each(1, 2 * SIDE, lambda t: scatter_corner(t).start())
    each(1, 2 * SIDE, lambda t: scatter_corner(t).wait_recv())
    line = local[rank]
    for t in range(2 * SIDE - 1):
        line = line + corner_parts[t]
    column[x] = line
    each(1, SIDE, lambda t: along_column(t, x).start())
    each(1, SIDE, lambda t: along_column(t, (x + SIDE - t) % SIDE).wait_recv())
    line = column[0]
    for t in range(1, SIDE):
        line = line + column[t]
    levels[z] = line
    each(1, height, lambda t: across(t, z).start())
    each(1, height, lambda t: across(t, (z + height - t) % height).wait_recv())
    line = levels[0]
    for t in range(1, height):
        line = line + levels[t]
    pieces[rank] = line
    each(1, 2 * SIDE, lambda t: gather_corner(t, rank).start())
    each(1, 2 * SIDE, lambda t: gather_corner(t, (rank + 2 * SIDE - t) % (2 * SIDE)).wait_recv())
    for r in range(2 * SIDE):
        gram[r * width : (r + 1) * width] = pieces[r]

    first_down.wait_send()
    for slot in range(SIDE):
        next_down(slot).wait_send()
    for dy in range(1, SIDE):
        side(SIDE - 1, dy).wait_send()
    for k in (1, 2, 3, 5, 7):
        back_copy(k, raised.at[2]).wait_send()
    for which in range(3):
        up(which, raised.at[which]).wait_send()
    part_copy.wait_send()
    each(1, 2 * SIDE, lambda t: scatter_corner(t).wait_send())
    each(1, SIDE, lambda t: along_column(t, x).wait_send())
    each(1, height, lambda t: across(t, z).wait_send())
    each(1, 2 * SIDE, lambda t: gather_corner(t, rank).wait_send())


def field_and_gram(codes, panels, blocks):
    slots, keypts, half = blocks.shape
    univ = panels.shape[2]
    height = lax.axis_size("img") // PLANE
    line = 2 * SIDE
    width = univ // line
    dma = pltpu.SemaphoreType.DMA
    return pl.pallas_call(
        field_kernel,
        out_shape=(
            jax.ShapeDtypeStruct(panels.shape, jnp.float32),
            jax.ShapeDtypeStruct((univ, univ), jnp.float32),
        ),
        in_specs=[
            pl.BlockSpec(memory_space=pltpu.SMEM),
            pl.BlockSpec(memory_space=pltpu.VMEM),
            pl.BlockSpec(memory_space=pl.ANY),
        ],
        out_specs=(
            pl.BlockSpec(memory_space=pltpu.VMEM),
            pl.BlockSpec(memory_space=pltpu.VMEM),
        ),
        scratch_shapes=[
            pltpu.VMEM((slots, keypts, half), jnp.bfloat16),
            pltpu.VMEM((2 * SIDE + 3, half, univ), jnp.bfloat16),
            pltpu.VMEM((2 * SIDE + 3, half, univ), jnp.bfloat16),
            pltpu.VMEM((2, half, univ), jnp.bfloat16),
            pltpu.VMEM((3, univ, keypts), jnp.bfloat16),
            pltpu.VMEM((BAND, 2, half, univ), jnp.bfloat16),
            pltpu.VMEM((BAND - 1, 2, half, univ), jnp.bfloat16),
            pltpu.VMEM((3, 2, half, univ), jnp.float32),
            pltpu.VMEM((3, 2, half, univ), jnp.bfloat16),
            pltpu.VMEM((3, 2, half, univ), jnp.bfloat16),
            pltpu.VMEM((2, half, 2 * univ), jnp.float32),
            pltpu.VMEM((half, 2 * univ), jnp.float32),
            pltpu.VMEM((line, width, univ), jnp.float32),
            pltpu.VMEM((line - 1, width, univ), jnp.float32),
            pltpu.VMEM((SIDE, width, univ), jnp.float32),
            pltpu.VMEM((height, width, univ), jnp.float32),
            pltpu.VMEM((line, width, univ), jnp.float32),
            dma((CHUNKS,)),
            dma((BAND,)),
            dma((BAND,)),
            dma,
            dma,
            dma((BAND - 1,)),
            dma((BAND - 1,)),
            dma((3,)),
            dma((3,)),
            dma,
            dma,
        ]
        + [dma((n - 1,)) for n in (line, SIDE, height, line) for _ in range(2)],
        compiler_params=pltpu.CompilerParams(
            collective_id=0, has_side_effects=True, vmem_limit_bytes=VMEM_LIMIT
        ),
        name="field",
    )(codes, panels, blocks)


def basis_kernel(scale, gram, field, basis):
    univ = gram.shape[0]
    left = gram[...] * scale
    rows = lax.broadcasted_iota(jnp.int32, (univ, univ), 0)
    columns = lax.broadcasted_iota(jnp.int32, (univ, univ), 1)
    right = (rows == columns).astype(jnp.float32)
    scales = jnp.zeros((univ, univ), jnp.float32)
    for j in range(0, univ, PIVOTS):
        top = (j // 8) * 8
        at = j - top
        low = left[top:]
        low_right = right[top:]
        low_rows = rows[top:]
        unit = [[None] * PIVOTS for _ in range(PIVOTS)]
        pivots = []
        inverses = []
        for t in range(PIVOTS):
            entry = [
                jnp.broadcast_to(low[at + a : at + a + 1, j + t : j + t + 1], (1, univ))
                for a in range(t, PIVOTS)
            ]
            for u in range(t):
                for a in range(t, PIVOTS):
                    entry[a - t] = entry[a - t] - unit[a][u] * (unit[t][u] * pivots[u])
            pivots.append(entry[0])
            inverses.append(1.0 / entry[0])
            for a in range(t + 1, PIVOTS):
                unit[a][t] = entry[a - t] * inverses[t]
        row = []
        row_right = []
        factor = []
        for t in range(PIVOTS):
            one = low[at + t : at + t + 1]
            one_right = low_right[at + t : at + t + 1]
            column = jnp.broadcast_to(low[:, j + t : j + t + 1], low.shape)
            for u in range(t):
                one = one - unit[t][u] * row[u]
                one_right = one_right - unit[t][u] * row_right[u]
                column = column - factor[u] * (unit[t][u] * pivots[u])
            row.append(one)
            row_right.append(one_right)
            factor.append(column * inverses[t])
        below = low_rows >= j + PIVOTS
        for t in range(PIVOTS):
            share = jnp.where(below, factor[t], 0.0)
            low = low - share * row[t]
            low_right = low_right - share * row_right[t]
            scales = jnp.where(rows == j + t, lax.rsqrt(pivots[t]), scales)
        for t in range(1, PIVOTS):
            low_right = jnp.where(low_rows == j + t, row_right[t], low_right)
        left = jnp.concatenate([left[:top], low], axis=0) if top else low
        right = jnp.concatenate([right[:top], low_right], axis=0) if top else low_right
    inverse_factor = right * scales
    for image in range(field.shape[0]):
        basis[image] = lax.dot_general(
            field[image],
            inverse_factor,
            (((1,), (1,)), ((), ())),
            precision=lax.Precision.HIGHEST,
            preferred_element_type=jnp.float32,
        )


def shards(panels, blocks, pairs, counts):
    codes = pair_codes(pairs, counts)
    field, gram = field_and_gram(codes, panels, blocks)
    rows = lax.axis_size("img") * panels.shape[0] * lax.axis_size("rep") * panels.shape[1]
    return pl.pallas_call(
        functools.partial(basis_kernel, 1.0 / rows),
        out_shape=jax.ShapeDtypeStruct(panels.shape, jnp.float32),
        in_specs=[pl.BlockSpec(memory_space=pltpu.VMEM)] * 2,
        out_specs=pl.BlockSpec(memory_space=pltpu.VMEM),
        name="basis",
    )(gram, field)


def solution(mesh):
    in_specs = (P("img", "rep", None), P("img", None, "rep"), P("img", None), P("img"))
    out_specs = P("img", "rep", None)
    return jax.shard_map(shards, mesh=mesh, in_specs=in_specs, out_specs=out_specs, check_vma=False)
```

```python
import functools

import jax
import jax.numpy as jnp
from jax import lax
from jax.experimental import pallas as pl
from jax.experimental.pallas import tpu as pltpu
from jax.sharding import PartitionSpec as P

MESH = pl.DeviceIdType.MESH
BAND = 8
SIDE = 4
PLANE = SIDE * SIDE
PIVOTS = 4
EMPTY = 4
LANES = 128
ORDER = (6, 7, 5, 3, 1, 8, 2, 4)
CHUNKS = 8
VMEM_LIMIT = 60 * 1024 * 1024


def remote(src, dst, send_sem, recv_sem, img, rep):
    return pltpu.make_async_remote_copy(
        src_ref=src,
        dst_ref=dst,
        send_sem=send_sem,
        recv_sem=recv_sem,
        device_id=(img, rep),
        device_id_type=MESH,
    )


def pair_codes(pairs, scratch, live, own, devices, capacity):
    lanes = scratch.shape[1]
    slots = pairs.shape[1]
    scratch[...] = jnp.zeros_like(scratch)
    scratch[0:2, 0:slots] = pairs[...]
    first = scratch[0:1, :]
    second = scratch[1:2, :]
    across = lax.broadcasted_iota(jnp.int32, (lanes, lanes), 1)
    down = lax.broadcasted_iota(jnp.int32, (lanes, lanes), 0)
    offset = jnp.broadcast_to(((second >> 1) - own - 1) & (devices - 1), (lanes, lanes))
    before = (offset.T == offset) & (down < across) & (down < live)
    rank = jnp.sum(jnp.where(before, 1, 0), axis=0, keepdims=True)
    code = across * 8 + (first & 1) * 2 + (second & 1)
    target = jnp.where(across < live, offset * capacity + rank, lanes)
    hit = target.T == across
    return EMPTY + jnp.sum(jnp.where(hit, code.T - EMPTY, 0), axis=0, keepdims=True)


def each(first, last, act):
    def body(t, _):
        act(t)
        return 0

    lax.fori_loop(first, last, body, 0)


def field_kernel(
    counts,
    pairs,
    panels,
    blocks_hbm,
    field,
    gram,
    codes,
    code_row,
    pair_rows,
    blocks,
    far,
    beyond,
    near_other,
    near,
    turned,
    returned,
    sums,
    raised,
    lifted,
    part,
    part_other,
    local,
    corner_parts,
    column,
    levels,
    pieces,
    load_sem,
    code_sem,
    far_send,
    far_recv,
    near_send,
    near_recv,
    back_send,
    back_recv,
    up_send,
    up_recv,
    part_send,
    part_recv,
    s1,
    r1,
    s2,
    r2,
    s3,
    r3,
    s4,
    r4,
):
    me = lax.axis_index("img")
    rep = lax.axis_index("rep")
    devices = lax.axis_size("img")
    slots, keypts, half = blocks.shape
    univ = panels.shape[2]
    capacity = slots // BAND
    step = slots // CHUNKS
    height = devices // PLANE
    z = me // PLANE
    x = (me // SIDE) % SIDE
    y = me % SIDE
    above = (me + SIDE) % devices
    below = (me + devices - SIDE) % devices
    own_row = 2 * SIDE
    zero_row = 2 * SIDE + 2

    def read(q):
        code = codes[0, q]
        return code // 8, (code // 2) % 4, code % 2

    def load(chunk):
        rows = pl.ds(chunk * step, step)
        return pltpu.make_async_copy(blocks_hbm.at[rows], blocks.at[rows], load_sem.at[chunk])

    for chunk in range(CHUNKS):
        load(chunk).start()

    rank = y * 2 + rep

    def in_corner(t):
        other = (rank + t) % (2 * SIDE)
        return other, me - y + other // 2, other % 2

    def in_column(t):
        other = (x + t) % SIDE
        return other, z * PLANE + other * SIDE + y

    def in_levels(t):
        return ((z + t) % height) * PLANE + me % PLANE

    barrier = pltpu.get_barrier_semaphore()

    def greet(img, core):
        pl.semaphore_signal(barrier, inc=1, device_id=(img, core), device_id_type=MESH)

    def greet_corner(t):
        _, img, core = in_corner(t)
        greet(img, core)

    each(1, height, lambda t: greet(in_levels(t), rep))
    each(1, 2 * SIDE, greet_corner)
    each(1, SIDE, lambda t: greet(in_column(t)[1], rep))
    greet(above, rep)
    greet(below, rep)

    code_row[...] = pair_codes(pairs, pair_rows, counts[0], me, devices, capacity)
    code_copy = pltpu.make_async_copy(code_row, codes, code_sem)
    code_copy.start()

    here = pl.ds(pl.multiple_of(rep * half, half), half)
    there = pl.ds(pl.multiple_of((1 - rep) * half, half), half)
    for image in range(2):
        far[own_row + image] = panels[image].astype(far.dtype)
        near[image, :, here] = panels[image].T.astype(near.dtype)
    far[zero_row] = jnp.zeros((half, univ), far.dtype)
    beyond[zero_row] = jnp.zeros((half, univ), far.dtype)
    near[2] = jnp.zeros((univ, keypts), near.dtype)

    pl.semaphore_wait(barrier, height - 1 + 2 * SIDE - 1 + SIDE - 1 + 2)

    def rows_of(buffer, slot):
        return buffer.at[pl.ds(2 * slot, 2)]

    def mate(dy):
        return me - y + (y + dy) % SIDE

    first_down = remote(
        rows_of(far, SIDE), rows_of(far, SIDE - 1), far_send.at[0], far_recv.at[SIDE - 1], below, rep
    )

    def next_down(slot):
        return remote(
            rows_of(far, slot),
            rows_of(beyond, slot),
            far_send.at[1 + slot],
            far_recv.at[SIDE + slot],
            below,
            rep,
        )

    def side(source, dy):
        slot = SIDE - 1 - dy
        return remote(
            rows_of(far, source),
            rows_of(far, slot),
            far_send.at[SIDE + dy],
            far_recv.at[slot],
            mate(dy),
            rep,
        )

    near_copy = remote(rows_of(far, SIDE), near_other, near_send, near_recv, me, 1 - rep)
    near_copy.start()
    first_down.start()
    for dy in range(1, SIDE):

        @pl.when(y + dy >= SIDE)
        def _():
            side(SIDE, dy).start()

    near_copy.wait()
    code_copy.wait()
    for image in range(2):
        near[image, :, there] = near_other[image].astype(jnp.float32).T.astype(near.dtype)
    for chunk in range(CHUNKS):
        load(chunk).wait()

    def back_copy(k, source):
        return remote(
            source,
            returned.at[k - 1],
            back_send.at[k - 1],
            back_recv.at[k - 1],
            mate(k % SIDE),
            rep,
        )

    def up(which, source):
        return remote(source, lifted.at[which], up_send.at[which], up_recv.at[which], above, rep)

    def reverse(t):
        k = ORDER[-1]
        for at in range(BAND - 1):
            k = jnp.where(t == at, ORDER[at], k)
        totals = [jnp.zeros((univ, half), jnp.float32) for _ in range(2)]
        for r in range(capacity):
            slot, first, second = read((k - 1) * capacity + r)
            product = jnp.dot(near[first], blocks[slot], preferred_element_type=jnp.float32)
            product = product.astype(jnp.bfloat16).astype(jnp.float32)
            share = second.astype(jnp.float32)
            totals[0] = totals[0] + product * (1.0 - share)
            totals[1] = totals[1] + product * share
        for image in range(2):
            turned[k - 1, image] = totals[image].T.astype(turned.dtype)

        @pl.when(k == 6)
        def _():
            up(2, turned.at[k - 1]).start()

    each(0, BAND, reverse)

    def far_wait(slot):
        remote(
            rows_of(far, SIDE - 1),
            rows_of(far, SIDE - 1),
            far_send.at[0],
            far_recv.at[slot],
            below,
            rep,
        ).wait_recv()

    far_wait(SIDE - 1)
    next_down(SIDE - 1).start()
    for dy in range(1, SIDE):

        @pl.when(y + dy < SIDE)
        def _():
            side(SIDE - 1, dy).start()

    for k in (7, 5, 3, 1):
        back_copy(k, turned.at[k - 1]).start()
    up(2, raised.at[2]).wait_recv()
    for image in range(2):
        value = turned[1, image].astype(jnp.float32) + lifted[2, image].astype(jnp.float32)
        raised[2, image] = value.astype(raised.dtype)
    back_copy(2, raised.at[2]).start()
    for slot in range(SIDE - 2, -1, -1):
        far_wait(slot)
        next_down(slot).start()

    def add(slot, source, k):
        for image in range(2):
            sums[slot, image] += source[k, image].astype(jnp.float32)

    def lift(slot, which):
        for image in range(2):
            raised[which, image] = sums[slot, image].astype(raised.dtype)
        up(which, raised.at[which]).start()

    def back_wait(k):
        back_copy(k, raised.at[2]).wait_recv()

    for image in range(2):
        sums[0, image] = jnp.zeros((half, univ), jnp.float32)
        sums[1, image] = turned[3, image].astype(jnp.float32)
        sums[2, image] = turned[7, image].astype(jnp.float32)

    for dy in (3, 1):
        back_wait(4 + dy)
        add(jnp.where(y >= dy, 1, 2), returned, 3 + dy)
    lift(2, 0)

    group = 8

    def forward(rows, out, panel_buffer, offset, first_group):
        def one(g):
            left = []
            right = []
            for r in range(group):
                place = g * group + r
                slot, first, second = read(offset * capacity + place)
                row = (place // capacity) * 2 + second
                left.append(blocks[slot, rows, :])
                right.append(
                    jnp.concatenate(
                        [
                            panel_buffer[jnp.where(first == image, row, zero_row)]
                            for image in range(2)
                        ],
                        axis=1,
                    )
                )
            out[...] += jnp.dot(
                jnp.concatenate(left, axis=1),
                jnp.concatenate(right, axis=0),
                preferred_element_type=jnp.float32,
            )

        if first_group:
            out[...] = jnp.zeros_like(out)
        each(0, SIDE * capacity // group, one)

    part_copy = remote(part.at[0], part_other, part_send, part_recv, me, 1 - rep)
    forward(there, part.at[0], far, 0, True)
    forward(here, part.at[1], far, 0, True)

    for dy in range(1, SIDE):
        back_wait(dy)
        add(jnp.where(y >= dy, 0, 1), returned, dy - 1)
    up(0, raised.at[0]).wait_recv()
    add(1, lifted, 0)
    lift(1, 1)

    for slot in range(SIDE, BAND):
        far_wait(slot)
    forward(there, part.at[0], beyond, SIDE, False)
    part_copy.start()
    forward(here, part.at[1], beyond, SIDE, False)
    part_copy.wait_recv()
    up(1, raised.at[1]).wait_recv()

    total = jnp.zeros((univ, univ), jnp.float32)
    for image in range(2):
        columns = pl.ds(image * univ, univ)
        value = panels[image] + part[1, :, columns] + part_other[:, columns]
        value = value + sums[0, image] + lifted[1, image].astype(jnp.float32)
        field[image] = value
        total = total + lax.dot_general(
            value,
            value,
            (((0,), (0,)), ((), ())),
            precision=lax.Precision.HIGHEST,
            preferred_element_type=jnp.float32,
        )

    width = local.shape[1]
    for r in range(2 * SIDE):
        local[r] = total[r * width : (r + 1) * width]

    def scatter_corner(t):
        other, img, core = in_corner(t)
        return remote(local.at[other], corner_parts.at[t - 1], s1.at[t - 1], r1.at[t - 1], img, core)

    def along_column(t, source):
        _, img = in_column(t)
        return remote(column.at[source], column.at[source], s2.at[t - 1], r2.at[t - 1], img, rep)

    def across(t, source):
        return remote(
            levels.at[source], levels.at[source], s3.at[t - 1], r3.at[t - 1], in_levels(t), rep
        )

    def gather_corner(t, source):
        _, img, core = in_corner(t)
        return remote(
            pieces.at[source], pieces.at[source], s4.at[t - 1], r4.at[t - 1], img, core
        )

    each(1, 2 * SIDE, lambda t: scatter_corner(t).start())
    each(1, 2 * SIDE, lambda t: scatter_corner(t).wait_recv())
    line = local[rank]
    for t in range(2 * SIDE - 1):
        line = line + corner_parts[t]
    column[x] = line
    each(1, SIDE, lambda t: along_column(t, x).start())
    each(1, SIDE, lambda t: along_column(t, (x + SIDE - t) % SIDE).wait_recv())
    line = column[0]
    for t in range(1, SIDE):
        line = line + column[t]
    levels[z] = line
    each(1, height, lambda t: across(t, z).start())
    each(1, height, lambda t: across(t, (z + height - t) % height).wait_recv())
    line = levels[0]
    for t in range(1, height):
        line = line + levels[t]
    pieces[rank] = line
    each(1, 2 * SIDE, lambda t: gather_corner(t, rank).start())
    each(1, 2 * SIDE, lambda t: gather_corner(t, (rank + 2 * SIDE - t) % (2 * SIDE)).wait_recv())
    for r in range(2 * SIDE):
        gram[r * width : (r + 1) * width] = pieces[r]

    first_down.wait_send()
    for slot in range(SIDE):
        next_down(slot).wait_send()
    for dy in range(1, SIDE):
        side(SIDE - 1, dy).wait_send()
    for k in (1, 2, 3, 5, 7):
        back_copy(k, raised.at[2]).wait_send()
    for which in range(3):
        up(which, raised.at[which]).wait_send()
    part_copy.wait_send()
    each(1, 2 * SIDE, lambda t: scatter_corner(t).wait_send())
    each(1, SIDE, lambda t: along_column(t, x).wait_send())
    each(1, height, lambda t: across(t, z).wait_send())
    each(1, 2 * SIDE, lambda t: gather_corner(t, rank).wait_send())


def field_and_gram(counts, pairs, panels, blocks):
    slots, keypts, half = blocks.shape
    univ = panels.shape[2]
    height = lax.axis_size("img") // PLANE
    line = 2 * SIDE
    width = univ // line
    dma = pltpu.SemaphoreType.DMA
    return pl.pallas_call(
        field_kernel,
        out_shape=(
            jax.ShapeDtypeStruct(panels.shape, jnp.float32),
            jax.ShapeDtypeStruct((univ, univ), jnp.float32),
        ),
        in_specs=[
            pl.BlockSpec(memory_space=pltpu.SMEM),
            pl.BlockSpec(memory_space=pltpu.VMEM),
            pl.BlockSpec(memory_space=pltpu.VMEM),
            pl.BlockSpec(memory_space=pl.ANY),
        ],
        out_specs=(
            pl.BlockSpec(memory_space=pltpu.VMEM),
            pl.BlockSpec(memory_space=pltpu.VMEM),
        ),
        scratch_shapes=[
            pltpu.SMEM((1, LANES), jnp.int32),
            pltpu.VMEM((1, LANES), jnp.int32),
            pltpu.VMEM((8, LANES), jnp.int32),
            pltpu.VMEM((slots, keypts, half), jnp.bfloat16),
            pltpu.VMEM((2 * SIDE + 3, half, univ), jnp.bfloat16),
            pltpu.VMEM((2 * SIDE + 3, half, univ), jnp.bfloat16),
            pltpu.VMEM((2, half, univ), jnp.bfloat16),
            pltpu.VMEM((3, univ, keypts), jnp.bfloat16),
            pltpu.VMEM((BAND, 2, half, univ), jnp.bfloat16),
            pltpu.VMEM((BAND - 1, 2, half, univ), jnp.bfloat16),
            pltpu.VMEM((3, 2, half, univ), jnp.float32),
            pltpu.VMEM((3, 2, half, univ), jnp.bfloat16),
            pltpu.VMEM((3, 2, half, univ), jnp.bfloat16),
            pltpu.VMEM((2, half, 2 * univ), jnp.float32),
            pltpu.VMEM((half, 2 * univ), jnp.float32),
            pltpu.VMEM((line, width, univ), jnp.float32),
            pltpu.VMEM((line - 1, width, univ), jnp.float32),
            pltpu.VMEM((SIDE, width, univ), jnp.float32),
            pltpu.VMEM((height, width, univ), jnp.float32),
            pltpu.VMEM((line, width, univ), jnp.float32),
            dma((CHUNKS,)),
            dma,
            dma((BAND,)),
            dma((BAND,)),
            dma,
            dma,
            dma((BAND - 1,)),
            dma((BAND - 1,)),
            dma((3,)),
            dma((3,)),
            dma,
            dma,
        ]
        + [dma((n - 1,)) for n in (line, SIDE, height, line) for _ in range(2)],
        compiler_params=pltpu.CompilerParams(
            collective_id=0, has_side_effects=True, vmem_limit_bytes=VMEM_LIMIT
        ),
        name="field",
    )(counts, pairs, panels, blocks)


def basis_kernel(scale, gram, field, basis):
    univ = gram.shape[0]
    left = gram[...] * scale
    rows = lax.broadcasted_iota(jnp.int32, (univ, univ), 0)
    columns = lax.broadcasted_iota(jnp.int32, (univ, univ), 1)
    right = (rows == columns).astype(jnp.float32)
    scales = jnp.zeros((univ, univ), jnp.float32)
    for j in range(0, univ, PIVOTS):
        top = (j // 8) * 8
        at = j - top
        low = left[top:]
        low_right = right[top:]
        low_rows = rows[top:]
        unit = [[None] * PIVOTS for _ in range(PIVOTS)]
        pivots = []
        inverses = []
        for t in range(PIVOTS):
            entry = [
                jnp.broadcast_to(low[at + a : at + a + 1, j + t : j + t + 1], (1, univ))
                for a in range(t, PIVOTS)
            ]
            for u in range(t):
                for a in range(t, PIVOTS):
                    entry[a - t] = entry[a - t] - unit[a][u] * (unit[t][u] * pivots[u])
            pivots.append(entry[0])
            inverses.append(1.0 / entry[0])
            for a in range(t + 1, PIVOTS):
                unit[a][t] = entry[a - t] * inverses[t]
        row = []
        row_right = []
        factor = []
        for t in range(PIVOTS):
            one = low[at + t : at + t + 1]
            one_right = low_right[at + t : at + t + 1]
            column = jnp.broadcast_to(low[:, j + t : j + t + 1], low.shape)
            for u in range(t):
                one = one - unit[t][u] * row[u]
                one_right = one_right - unit[t][u] * row_right[u]
                column = column - factor[u] * (unit[t][u] * pivots[u])
            row.append(one)
            row_right.append(one_right)
            factor.append(column * inverses[t])
        below = low_rows >= j + PIVOTS
        for t in range(PIVOTS):
            share = jnp.where(below, factor[t], 0.0)
            low = low - share * row[t]
            low_right = low_right - share * row_right[t]
            scales = jnp.where(rows == j + t, lax.rsqrt(pivots[t]), scales)
        for t in range(1, PIVOTS):
            low_right = jnp.where(low_rows == j + t, row_right[t], low_right)
        left = jnp.concatenate([left[:top], low], axis=0) if top else low
        right = jnp.concatenate([right[:top], low_right], axis=0) if top else low_right
    inverse_factor = right * scales
    for image in range(field.shape[0]):
        basis[image] = lax.dot_general(
            field[image],
            inverse_factor,
            (((1,), (1,)), ((), ())),
            precision=lax.Precision.HIGHEST,
            preferred_element_type=jnp.float32,
        )


def shards(panels, blocks, pairs, counts):
    field, gram = field_and_gram(counts, pairs.T, panels, blocks)
    rows = lax.axis_size("img") * panels.shape[0] * lax.axis_size("rep") * panels.shape[1]
    return pl.pallas_call(
        functools.partial(basis_kernel, 1.0 / rows),
        out_shape=jax.ShapeDtypeStruct(panels.shape, jnp.float32),
        in_specs=[pl.BlockSpec(memory_space=pltpu.VMEM)] * 2,
        out_specs=pl.BlockSpec(memory_space=pltpu.VMEM),
        name="basis",
    )(gram, field)


def solution(mesh):
    in_specs = (P("img", "rep", None), P("img", None, "rep"), P("img", None), P("img"))
    out_specs = P("img", "rep", None)
    return jax.shard_map(shards, mesh=mesh, in_specs=in_specs, out_specs=out_specs, check_vma=False)
```

```python
import functools

import jax
import jax.numpy as jnp
from jax import lax
from jax.experimental import pallas as pl
from jax.experimental.pallas import tpu as pltpu
from jax.sharding import PartitionSpec as P

MESH = pl.DeviceIdType.MESH
BAND = 8
SIDE = 4
PLANE = SIDE * SIDE
PIVOTS = 4
EMPTY = 4
LANES = 128
ORDER = (6, 7, 5, 8, 3, 1, 2, 4)
CHUNKS = 8
VMEM_LIMIT = 60 * 1024 * 1024


def remote(src, dst, send_sem, recv_sem, img, rep):
    return pltpu.make_async_remote_copy(
        src_ref=src,
        dst_ref=dst,
        send_sem=send_sem,
        recv_sem=recv_sem,
        device_id=(img, rep),
        device_id_type=MESH,
    )


def pair_codes(pairs, scratch, live, own, devices, capacity):
    lanes = scratch.shape[1]
    slots = pairs.shape[1]
    scratch[...] = jnp.zeros_like(scratch)
    scratch[0:2, 0:slots] = pairs[...]
    first = scratch[0:1, :]
    second = scratch[1:2, :]
    across = lax.broadcasted_iota(jnp.int32, (lanes, lanes), 1)
    down = lax.broadcasted_iota(jnp.int32, (lanes, lanes), 0)
    offset = jnp.broadcast_to(((second >> 1) - own - 1) & (devices - 1), (lanes, lanes))
    before = (offset.T == offset) & (down < across) & (down < live)
    rank = jnp.sum(jnp.where(before, 1, 0), axis=0, keepdims=True)
    code = across * 8 + (first & 1) * 2 + (second & 1)
    target = jnp.where(across < live, offset * capacity + rank, lanes)
    hit = target.T == across
    return EMPTY + jnp.sum(jnp.where(hit, code.T - EMPTY, 0), axis=0, keepdims=True)


def each(first, last, act):
    def body(t, _):
        act(t)
        return 0

    lax.fori_loop(first, last, body, 0)


def field_kernel(
    counts,
    pairs,
    panels,
    blocks_hbm,
    field,
    gram,
    codes,
    code_row,
    pair_rows,
    blocks,
    far,
    beyond,
    near_other,
    near,
    turned,
    returned,
    sums,
    raised,
    lifted,
    part,
    part_other,
    local,
    corner_parts,
    column,
    levels,
    pieces,
    load_sem,
    code_sem,
    far_send,
    far_recv,
    near_send,
    near_recv,
    back_send,
    back_recv,
    up_send,
    up_recv,
    part_send,
    part_recv,
    s1,
    r1,
    s2,
    r2,
    s3,
    r3,
    s4,
    r4,
):
    me = lax.axis_index("img")
    rep = lax.axis_index("rep")
    devices = lax.axis_size("img")
    slots, keypts, half = blocks.shape
    univ = panels.shape[2]
    capacity = slots // BAND
    step = slots // CHUNKS
    height = devices // PLANE
    z = me // PLANE
    x = (me // SIDE) % SIDE
    y = me % SIDE
    above = (me + SIDE) % devices
    below = (me + devices - SIDE) % devices
    own_row = 2 * SIDE
    zero_row = 2 * SIDE + 2

    def read(q):
        code = codes[0, q]
        return code // 8, (code // 2) % 4, code % 2

    def load(chunk):
        rows = pl.ds(chunk * step, step)
        return pltpu.make_async_copy(blocks_hbm.at[rows], blocks.at[rows], load_sem.at[chunk])

    for chunk in range(CHUNKS):
        load(chunk).start()

    rank = y * 2 + rep

    def in_corner(t):
        other = (rank + t) % (2 * SIDE)
        return other, me - y + other // 2, other % 2

    def in_column(t):
        other = (x + t) % SIDE
        return other, z * PLANE + other * SIDE + y

    def in_levels(t):
        return ((z + t) % height) * PLANE + me % PLANE

    barrier = pltpu.get_barrier_semaphore()

    def greet(img, core):
        pl.semaphore_signal(barrier, inc=1, device_id=(img, core), device_id_type=MESH)

    def greet_corner(t):
        _, img, core = in_corner(t)
        greet(img, core)

    each(1, height, lambda t: greet(in_levels(t), rep))
    each(1, 2 * SIDE, greet_corner)
    each(1, SIDE, lambda t: greet(in_column(t)[1], rep))
    greet(above, rep)
    greet(below, rep)

    code_row[...] = pair_codes(pairs, pair_rows, counts[0], me, devices, capacity)
    code_copy = pltpu.make_async_copy(code_row, codes, code_sem)
    code_copy.start()

    here = pl.ds(pl.multiple_of(rep * half, half), half)
    there = pl.ds(pl.multiple_of((1 - rep) * half, half), half)
    for image in range(2):
        far[own_row + image] = panels[image].astype(far.dtype)
        near[image, :, here] = panels[image].T.astype(near.dtype)
    far[zero_row] = jnp.zeros((half, univ), far.dtype)
    beyond[zero_row] = jnp.zeros((half, univ), far.dtype)
    near[2] = jnp.zeros((univ, keypts), near.dtype)

    pl.semaphore_wait(barrier, height - 1 + 2 * SIDE - 1 + SIDE - 1 + 2)

    def rows_of(buffer, slot):
        return buffer.at[pl.ds(2 * slot, 2)]

    def mate(dy):
        return me - y + (y + dy) % SIDE

    def first_down(image):
        return remote(
            far.at[own_row + image],
            far.at[2 * SIDE - 2 + image],
            far_send.at[image],
            far_recv.at[2 * SIDE - 2 + image],
            below,
            rep,
        )

    def next_down(slot, image):
        return remote(
            far.at[2 * slot + image],
            beyond.at[2 * slot + image],
            far_send.at[2 + 2 * slot + image],
            far_recv.at[2 * SIDE + 2 * slot + image],
            below,
            rep,
        )

    def side(source, dy, image):
        slot = SIDE - 1 - dy
        return remote(
            far.at[2 * source + image],
            far.at[2 * slot + image],
            far_send.at[2 * SIDE + 2 * dy + image],
            far_recv.at[2 * slot + image],
            mate(dy),
            rep,
        )

    near_copy = remote(rows_of(far, SIDE), near_other, near_send, near_recv, me, 1 - rep)
    near_copy.start()
    for image in range(2):
        first_down(image).start()
    for image in range(2):
        for dy in range(1, SIDE):

            @pl.when(y + dy >= SIDE)
            def _():
                side(SIDE, dy, image).start()

    near_copy.wait()
    code_copy.wait()
    for image in range(2):
        near[image, :, there] = near_other[image].astype(jnp.float32).T.astype(near.dtype)
    for chunk in range(CHUNKS):
        load(chunk).wait()

    def back_copy(k, source):
        return remote(
            source,
            returned.at[k - 1],
            back_send.at[k - 1],
            back_recv.at[k - 1],
            mate(k % SIDE),
            rep,
        )

    def up(which, source):
        return remote(source, lifted.at[which], up_send.at[which], up_recv.at[which], above, rep)

    def reverse(t):
        k = ORDER[-1]
        for at in range(BAND - 1):
            k = jnp.where(t == at, ORDER[at], k)
        totals = [jnp.zeros((univ, half), jnp.float32) for _ in range(2)]
        for r in range(capacity):
            slot, first, second = read((k - 1) * capacity + r)
            product = jnp.dot(near[first], blocks[slot], preferred_element_type=jnp.float32)
            product = product.astype(jnp.bfloat16).astype(jnp.float32)
            share = second.astype(jnp.float32)
            totals[0] = totals[0] + product * (1.0 - share)
            totals[1] = totals[1] + product * share
        for image in range(2):
            turned[k - 1, image] = totals[image].T.astype(turned.dtype)

        @pl.when(k == 6)
        def _():
            up(2, turned.at[k - 1]).start()

    def far_wait(slot, image):
        remote(
            far.at[2 * SIDE - 2],
            far.at[2 * SIDE - 2],
            far_send.at[0],
            far_recv.at[2 * slot + image],
            below,
            rep,
        ).wait_recv()

    each(0, BAND // 2, reverse)
    for k in (7, 5):
        back_copy(k, turned.at[k - 1]).start()
    for image in range(2):
        far_wait(SIDE - 1, image)
        for dy in range(1, SIDE):

            @pl.when(y + dy < SIDE)
            def _():
                side(SIDE - 1, dy, image).start()

        next_down(SIDE - 1, image).start()
    each(BAND // 2, BAND, reverse)
    for k in (3, 1):
        back_copy(k, turned.at[k - 1]).start()
    up(2, raised.at[2]).wait_recv()
    for image in range(2):
        value = turned[1, image].astype(jnp.float32) + lifted[2, image].astype(jnp.float32)
        raised[2, image] = value.astype(raised.dtype)
    back_copy(2, raised.at[2]).start()
    for slot in range(SIDE - 2, -1, -1):
        for image in range(2):
            far_wait(slot, image)
            next_down(slot, image).start()

    def add(slot, source, k):
        for image in range(2):
            sums[slot, image] += source[k, image].astype(jnp.float32)

    def lift(slot, which):
        for image in range(2):
            raised[which, image] = sums[slot, image].astype(raised.dtype)
        up(which, raised.at[which]).start()

    def back_wait(k):
        back_copy(k, raised.at[2]).wait_recv()

    for image in range(2):
        sums[0, image] = jnp.zeros((half, univ), jnp.float32)
        sums[1, image] = turned[3, image].astype(jnp.float32)
        sums[2, image] = turned[7, image].astype(jnp.float32)

    for dy in (3, 1):
        back_wait(4 + dy)
        add(jnp.where(y >= dy, 1, 2), returned, 3 + dy)
    lift(2, 0)

    group = 8

    def forward(rows, out, panel_buffer, offset, first_group):
        def one(g):
            left = []
            right = []
            for r in range(group):
                place = g * group + r
                slot, first, second = read(offset * capacity + place)
                row = (place // capacity) * 2 + second
                left.append(blocks[slot, rows, :])
                right.append(
                    jnp.concatenate(
                        [
                            panel_buffer[jnp.where(first == image, row, zero_row)]
                            for image in range(2)
                        ],
                        axis=1,
                    )
                )
            out[...] += jnp.dot(
                jnp.concatenate(left, axis=1),
                jnp.concatenate(right, axis=0),
                preferred_element_type=jnp.float32,
            )

        if first_group:
            out[...] = jnp.zeros_like(out)
        each(0, SIDE * capacity // group, one)

    part_copy = remote(part.at[0], part_other, part_send, part_recv, me, 1 - rep)
    forward(there, part.at[0], far, 0, True)
    forward(here, part.at[1], far, 0, True)

    for dy in range(1, SIDE):
        back_wait(dy)
        add(jnp.where(y >= dy, 0, 1), returned, dy - 1)
    up(0, raised.at[0]).wait_recv()
    add(1, lifted, 0)
    lift(1, 1)

    for slot in range(SIDE, BAND):
        for image in range(2):
            far_wait(slot, image)
    forward(there, part.at[0], beyond, SIDE, False)
    part_copy.start()
    forward(here, part.at[1], beyond, SIDE, False)
    part_copy.wait_recv()
    up(1, raised.at[1]).wait_recv()

    total = jnp.zeros((univ, univ), jnp.float32)
    for image in range(2):
        columns = pl.ds(image * univ, univ)
        value = panels[image] + part[1, :, columns] + part_other[:, columns]
        value = value + sums[0, image] + lifted[1, image].astype(jnp.float32)
        field[image] = value
        total = total + lax.dot_general(
            value,
            value,
            (((0,), (0,)), ((), ())),
            precision=lax.Precision.HIGHEST,
            preferred_element_type=jnp.float32,
        )

    width = local.shape[1]
    for r in range(2 * SIDE):
        local[r] = total[r * width : (r + 1) * width]

    def scatter_corner(t):
        other, img, core = in_corner(t)
        return remote(local.at[other], corner_parts.at[t - 1], s1.at[t - 1], r1.at[t - 1], img, core)

    def along_column(t, source):
        _, img = in_column(t)
        return remote(column.at[source], column.at[source], s2.at[t - 1], r2.at[t - 1], img, rep)

    def across(t, source):
        return remote(
            levels.at[source], levels.at[source], s3.at[t - 1], r3.at[t - 1], in_levels(t), rep
        )

    def gather_corner(t, source):
        _, img, core = in_corner(t)
        return remote(
            pieces.at[source], pieces.at[source], s4.at[t - 1], r4.at[t - 1], img, core
        )

    each(1, 2 * SIDE, lambda t: scatter_corner(t).start())
    each(1, 2 * SIDE, lambda t: scatter_corner(t).wait_recv())
    line = local[rank]
    for t in range(2 * SIDE - 1):
        line = line + corner_parts[t]
    column[x] = line
    each(1, SIDE, lambda t: along_column(t, x).start())
    each(1, SIDE, lambda t: along_column(t, (x + SIDE - t) % SIDE).wait_recv())
    line = column[0]
    for t in range(1, SIDE):
        line = line + column[t]
    levels[z] = line
    each(1, height, lambda t: across(t, z).start())
    each(1, height, lambda t: across(t, (z + height - t) % height).wait_recv())
    line = levels[0]
    for t in range(1, height):
        line = line + levels[t]
    pieces[rank] = line
    each(1, 2 * SIDE, lambda t: gather_corner(t, rank).start())
    each(1, 2 * SIDE, lambda t: gather_corner(t, (rank + 2 * SIDE - t) % (2 * SIDE)).wait_recv())
    for r in range(2 * SIDE):
        gram[r * width : (r + 1) * width] = pieces[r]

    for image in range(2):
        first_down(image).wait_send()
        for slot in range(SIDE):
            next_down(slot, image).wait_send()
        for dy in range(1, SIDE):
            side(SIDE - 1, dy, image).wait_send()
    for k in (1, 2, 3, 5, 7):
        back_copy(k, raised.at[2]).wait_send()
    for which in range(3):
        up(which, raised.at[which]).wait_send()
    part_copy.wait_send()
    each(1, 2 * SIDE, lambda t: scatter_corner(t).wait_send())
    each(1, SIDE, lambda t: along_column(t, x).wait_send())
    each(1, height, lambda t: across(t, z).wait_send())
    each(1, 2 * SIDE, lambda t: gather_corner(t, rank).wait_send())


def field_and_gram(counts, pairs, panels, blocks):
    slots, keypts, half = blocks.shape
    univ = panels.shape[2]
    height = lax.axis_size("img") // PLANE
    line = 2 * SIDE
    width = univ // line
    dma = pltpu.SemaphoreType.DMA
    return pl.pallas_call(
        field_kernel,
        out_shape=(
            jax.ShapeDtypeStruct(panels.shape, jnp.float32),
            jax.ShapeDtypeStruct((univ, univ), jnp.float32),
        ),
        in_specs=[
            pl.BlockSpec(memory_space=pltpu.SMEM),
            pl.BlockSpec(memory_space=pltpu.VMEM),
            pl.BlockSpec(memory_space=pltpu.VMEM),
            pl.BlockSpec(memory_space=pl.ANY),
        ],
        out_specs=(
            pl.BlockSpec(memory_space=pltpu.VMEM),
            pl.BlockSpec(memory_space=pltpu.VMEM),
        ),
        scratch_shapes=[
            pltpu.SMEM((1, LANES), jnp.int32),
            pltpu.VMEM((1, LANES), jnp.int32),
            pltpu.VMEM((8, LANES), jnp.int32),
            pltpu.VMEM((slots, keypts, half), jnp.bfloat16),
            pltpu.VMEM((2 * SIDE + 3, half, univ), jnp.bfloat16),
            pltpu.VMEM((2 * SIDE + 3, half, univ), jnp.bfloat16),
            pltpu.VMEM((2, half, univ), jnp.bfloat16),
            pltpu.VMEM((3, univ, keypts), jnp.bfloat16),
            pltpu.VMEM((BAND, 2, half, univ), jnp.bfloat16),
            pltpu.VMEM((BAND - 1, 2, half, univ), jnp.bfloat16),
            pltpu.VMEM((3, 2, half, univ), jnp.float32),
            pltpu.VMEM((3, 2, half, univ), jnp.bfloat16),
            pltpu.VMEM((3, 2, half, univ), jnp.bfloat16),
            pltpu.VMEM((2, half, 2 * univ), jnp.float32),
            pltpu.VMEM((half, 2 * univ), jnp.float32),
            pltpu.VMEM((line, width, univ), jnp.float32),
            pltpu.VMEM((line - 1, width, univ), jnp.float32),
            pltpu.VMEM((SIDE, width, univ), jnp.float32),
            pltpu.VMEM((height, width, univ), jnp.float32),
            pltpu.VMEM((line, width, univ), jnp.float32),
            dma((CHUNKS,)),
            dma,
            dma((2 * BAND,)),
            dma((2 * BAND,)),
            dma,
            dma,
            dma((BAND - 1,)),
            dma((BAND - 1,)),
            dma((3,)),
            dma((3,)),
            dma,
            dma,
        ]
        + [dma((n - 1,)) for n in (line, SIDE, height, line) for _ in range(2)],
        compiler_params=pltpu.CompilerParams(
            collective_id=0, has_side_effects=True, vmem_limit_bytes=VMEM_LIMIT
        ),
        name="field",
    )(counts, pairs, panels, blocks)


def basis_kernel(scale, gram, field, basis):
    univ = gram.shape[0]
    left = gram[...] * scale
    rows = lax.broadcasted_iota(jnp.int32, (univ, univ), 0)
    columns = lax.broadcasted_iota(jnp.int32, (univ, univ), 1)
    right = (rows == columns).astype(jnp.float32)
    scales = jnp.zeros((univ, univ), jnp.float32)
    for j in range(0, univ, PIVOTS):
        top = (j // 8) * 8
        at = j - top
        low = left[top:]
        low_right = right[top:]
        low_rows = rows[top:]
        unit = [[None] * PIVOTS for _ in range(PIVOTS)]
        pivots = []
        inverses = []
        for t in range(PIVOTS):
            entry = [
                jnp.broadcast_to(low[at + a : at + a + 1, j + t : j + t + 1], (1, univ))
                for a in range(t, PIVOTS)
            ]
            for u in range(t):
                for a in range(t, PIVOTS):
                    entry[a - t] = entry[a - t] - unit[a][u] * (unit[t][u] * pivots[u])
            pivots.append(entry[0])
            inverses.append(1.0 / entry[0])
            for a in range(t + 1, PIVOTS):
                unit[a][t] = entry[a - t] * inverses[t]
        row = []
        row_right = []
        factor = []
        for t in range(PIVOTS):
            one = low[at + t : at + t + 1]
            one_right = low_right[at + t : at + t + 1]
            column = jnp.broadcast_to(low[:, j + t : j + t + 1], low.shape)
            for u in range(t):
                one = one - unit[t][u] * row[u]
                one_right = one_right - unit[t][u] * row_right[u]
                column = column - factor[u] * (unit[t][u] * pivots[u])
            row.append(one)
            row_right.append(one_right)
            factor.append(column * inverses[t])
        below = low_rows >= j + PIVOTS
        for t in range(PIVOTS):
            share = jnp.where(below, factor[t], 0.0)
            low = low - share * row[t]
            low_right = low_right - share * row_right[t]
            scales = jnp.where(rows == j + t, lax.rsqrt(pivots[t]), scales)
        for t in range(1, PIVOTS):
            low_right = jnp.where(low_rows == j + t, row_right[t], low_right)
        left = jnp.concatenate([left[:top], low], axis=0) if top else low
        right = jnp.concatenate([right[:top], low_right], axis=0) if top else low_right
    inverse_factor = right * scales
    for image in range(field.shape[0]):
        basis[image] = lax.dot_general(
            field[image],
            inverse_factor,
            (((1,), (1,)), ((), ())),
            precision=lax.Precision.HIGHEST,
            preferred_element_type=jnp.float32,
        )


def shards(panels, blocks, pairs, counts):
    field, gram = field_and_gram(counts, pairs.T, panels, blocks)
    rows = lax.axis_size("img") * panels.shape[0] * lax.axis_size("rep") * panels.shape[1]
    return pl.pallas_call(
        functools.partial(basis_kernel, 1.0 / rows),
        out_shape=jax.ShapeDtypeStruct(panels.shape, jnp.float32),
        in_specs=[pl.BlockSpec(memory_space=pltpu.VMEM)] * 2,
        out_specs=pl.BlockSpec(memory_space=pltpu.VMEM),
        name="basis",
    )(gram, field)


def solution(mesh):
    in_specs = (P("img", "rep", None), P("img", None, "rep"), P("img", None), P("img"))
    out_specs = P("img", "rep", None)
    return jax.shard_map(shards, mesh=mesh, in_specs=in_specs, out_specs=out_specs, check_vma=False)
```
